256 devices in a mesh: head: 8 (over z), blk: 4 (over y_hi, core), quarter: 8 (over x, y_lo).
Axes of the slice: x: 4, y: 4 (y_hi: 2, y_lo: 2; y = y_hi * 2 + y_lo), z: 8, core: 2. Of those that a mesh axis runs over, the one named last changes fastest.
Arguments:
- queries: bfloat16 [256, 16384], P('blk', 'head'), may hold values from -64 to 64
- cache_keys: bfloat16 [65536, 8, 128], P(('blk', 'quarter'), 'head'), may hold values from -6 to 6
- cache_values: bfloat16 [65536, 8, 128], P(('blk', 'quarter'), 'head'), may hold values from -6 to 6
- step_keys: bfloat16 [256, 8, 128], P(None, 'head'), may hold values from -6 to 6
- step_values: bfloat16 [256, 8, 128], P(None, 'head'), may hold values from -6 to 6
- branch: int32 [16], replicated, may hold values from 16 to 65536, as said below
- out_weight: bfloat16 [16384, 16384], P('head', ('blk', 'quarter')), may hold values from -0.046875 to 0.046875
Outputs:
- projected: bfloat16 [256, 16384], P('head', ('blk', 'quarter'))
The draws below stay inside these ranges and needn't reach their ends.
Inputs may be any that keep to these rules, and one draw needn't show every extreme that they name: `branch`: some particle continues from the whole prompt of 65536 tokens.
All inputs are finite; a program needn't handle non-finite values.
Results may differ from the reference program's by a relative error of at most 0.018.
Values may be sent and summed in bfloat16 or wider, within the bound.
A program may use at most 64 MiB of HBM per device.

```python
from functools import partial
import jax
import jax.numpy as jnp
from jax import lax

D = 16384
QH = 128
KVH = 8
HD = 128
PARTICLES = 16
STEP = 16
TOKENS = 256
CTX = 65536


def draw_queries(key, part):
    base_key = jax.random.fold_in(key, 101)
    values = jnp.clip(3.0 * jax.random.normal(base_key, (TOKENS, QH * HD), jnp.float32), -15.0, 15.0)
    return values.astype(jnp.bfloat16)


def draw_cache_keys(key, part):
    base_key = jax.random.fold_in(key, 202)
    values = jnp.clip(jax.random.normal(base_key, (CTX, KVH, HD), jnp.float32), -5.5, 5.5)
    return values.astype(jnp.bfloat16)


def draw_branch(key, part):
    first_key = jax.random.fold_in(key, 11)
    second_key = jax.random.fold_in(key, 12)
    third_key = jax.random.fold_in(key, 13)
    root = jax.random.randint(first_key, (PARTICLES,), 0, CTX, dtype=jnp.int32)
    shifts = jax.random.randint(second_key, (PARTICLES,), 0, 19, dtype=jnp.int32)
    lengths = jnp.minimum(16 + jnp.right_shift(root, shifts), CTX)
    chosen = jax.random.randint(third_key, (), 0, PARTICLES, dtype=jnp.int32)
    return jnp.where(jnp.arange(PARTICLES, dtype=jnp.int32) == chosen, CTX, lengths).astype(jnp.int32)


def shard_levels(own_key, shape, split, smallest, largest):
    gain = 1.0
    for position, shards_of in split:
        steps = jax.random.uniform(jax.random.fold_in(jax.random.fold_in(own_key, 6), position), (shards_of,), jnp.float32, smallest / len(split), largest / len(split))
        gain = gain * jnp.repeat(jnp.exp(steps), shape[position] // shards_of).reshape((-1,) + (1,) * (len(shape) - 1 - position))
    return gain


def normal_values(rng, dims, scale, most, cuts=(), held_as=jnp.bfloat16):
    level = shard_levels(rng, dims, cuts, -0.22, 0.18) if cuts else 1.0
    values = jax.random.normal(rng, dims, jnp.float32) * scale * level
    return jnp.minimum(jnp.maximum(values, -most), most).astype(held_as)


def setup_inputs(seed: int = 0) -> dict:
    splits = jax.random.split(jax.random.key(seed), 8)
    return {
        "queries": draw_queries(jax.random.fold_in(splits[7], 71), 0),
        "cache_keys": draw_cache_keys(jax.random.fold_in(splits[7], 71), 0),
        "cache_values": normal_values(splits[2], (CTX, KVH, HD), 1.0, 6.0, ((0, 32), (1, 8))),
        "step_keys": normal_values(splits[3], (TOKENS, KVH, HD), 1.0, 6.0, ((1, 8),)),
        "step_values": normal_values(splits[4], (TOKENS, KVH, HD), 1.0, 6.0, ((1, 8),)),
        "branch": draw_branch(jax.random.fold_in(splits[7], 71), 0),
        "out_weight": normal_values(splits[6], (QH * HD, D), (QH * HD) ** -0.5, 0.046875, ((0, 8), (1, 32))),
    }


NEGATIVE = -1e30


def head_attention(inputs, branch):
    query_head, key_head, value_head, fresh_keys, fresh_values = inputs
    key_wide = key_head.astype(jnp.float32)
    value_wide = value_head.astype(jnp.float32)
    key_index = jnp.arange(CTX, dtype=jnp.int32)
    step_index = jnp.arange(STEP, dtype=jnp.int32)
    score_scale = HD ** -0.5

    def particle(pieces):
        query_rows, own_keys, own_values, limit = pieces
        query_wide = query_rows.astype(jnp.float32)
        visible = key_index < limit
        scores = jnp.einsum("tgd,cd->tgc", query_wide, key_wide) * score_scale
        scores = jnp.where(visible[None, None, :], scores, NEGATIVE)
        causal = step_index[None, :] <= step_index[:, None]
        fresh_scores = jnp.einsum("tgd,jd->tgj", query_wide, own_keys.astype(jnp.float32)) * score_scale
        fresh_scores = jnp.where(causal[:, None, :], fresh_scores, NEGATIVE)
        row_peak = jnp.maximum(jnp.max(scores, axis=-1), jnp.max(fresh_scores, axis=-1))
        weights = jnp.where(visible[None, None, :], jnp.exp(scores - row_peak[..., None]), 0.0)
        fresh_weights = jnp.where(causal[:, None, :], jnp.exp(fresh_scores - row_peak[..., None]), 0.0)
        weight_sum = jnp.sum(weights, axis=-1) + jnp.sum(fresh_weights, axis=-1)
        weighted = jnp.einsum("tgc,cd->tgd", weights.astype(jnp.bfloat16).astype(jnp.float32), value_wide)
        weighted = weighted + jnp.einsum("tgj,jd->tgd", fresh_weights.astype(jnp.bfloat16).astype(jnp.float32), own_values.astype(jnp.float32))
        return (weighted / weight_sum[..., None]).astype(jnp.bfloat16)

    return lax.map(particle, (query_head, fresh_keys, fresh_values, branch))


def reference(queries, cache_keys, cache_values, step_keys, step_values, branch, out_weight):
    group_size = QH // KVH
    query_heads = queries.reshape(PARTICLES, STEP, KVH, group_size, HD).transpose(2, 0, 1, 3, 4)
    key_heads = cache_keys.transpose(1, 0, 2)
    value_heads = cache_values.transpose(1, 0, 2)
    fresh_key_heads = step_keys.reshape(PARTICLES, STEP, KVH, HD).transpose(2, 0, 1, 3)
    fresh_value_heads = step_values.reshape(PARTICLES, STEP, KVH, HD).transpose(2, 0, 1, 3)
    outputs = lax.map(partial(head_attention, branch=branch), (query_heads, key_heads, value_heads, fresh_key_heads, fresh_value_heads))
    attended = outputs.transpose(1, 2, 0, 3, 4).reshape(TOKENS, QH * HD)
    return jnp.dot(attended, out_weight, preferred_element_type=jnp.float32).astype(jnp.bfloat16)
```

```python
import functools

import jax
import jax.numpy as jnp
from jax import lax
from jax.experimental import pallas as pl
from jax.experimental.pallas import tpu as pltpu
from jax.sharding import PartitionSpec as P

MESH = pl.DeviceIdType.MESH
NEGATIVE = -1e30
LOG2E = 1.4426950408889634
PARTICLES = 16
STEP = 16
GROUP = 16
HD = 128
WIDTH = GROUP * HD
HALF = WIDTH // 2
HEADS = 8
KEY_BLOCK = 512


def place():
    head = lax.axis_index("head")
    blk = lax.axis_index("blk")
    quarter = lax.axis_index("quarter")
    return head, quarter // 2, (blk // 2) * 2 + quarter % 2, blk % 2


def device(head, x, y, core):
    return (head, (y // 2) * 2 + core, x * 2 + y % 2)


def remote(src, dst, send, recv, to):
    return pltpu.make_async_remote_copy(
        src_ref=src,
        dst_ref=dst,
        send_sem=send,
        recv_sem=recv,
        device_id=to,
        device_id_type=MESH,
    )


def gather_kernel(mine, everyone, local_sem, send, recv):
    head, x, y, core = place()
    other = device(head, x, y, 1 - core)
    across = device(head, x, 3 - y, core)
    right = device(head, (x + 1) % 4, y, core)
    left = device(head, (x + 3) % 4, y, core)
    barrier = pltpu.get_barrier_semaphore()
    for peer in (other, across, right, left):
        pl.semaphore_signal(barrier, inc=1, device_id=peer, device_id_type=MESH)
    own_block = (y // 2) * 2 + core
    far_block = (1 - y // 2) * 2 + core
    keep = pltpu.make_async_copy(mine, everyone.at[own_block], local_sem)
    keep.start()
    pl.semaphore_wait(barrier, 4)

    first, second = x, (x + 2) % 4
    copies = []

    def begin(index, src, dst, to):
        copy = remote(src, dst, send.at[index], recv.at[index], to)
        copy.start()
        copies.append(copy)
        return copy

    direct = [
        begin(i, mine.at[piece], everyone.at[own_block, piece], across)
        for i, piece in enumerate((first, second))
    ]
    share = begin(2, mine, everyone.at[own_block], other)

    def arrived(piece):
        return everyone.at[far_block, piece]

    direct[0].wait_recv()
    to_right = begin(3, arrived(first), arrived(first), right)
    to_left = begin(4, arrived(first), arrived(first), left)
    forward = [begin(5, arrived(first), arrived(first), other)]
    direct[1].wait_recv()
    forward.append(begin(6, arrived(second), arrived(second), other))
    from_left, from_right = (x + 3) % 4, (x + 1) % 4
    to_right.wait_recv()
    forward.append(begin(7, arrived(from_left), arrived(from_left), other))
    to_left.wait_recv()
    forward.append(begin(8, arrived(from_right), arrived(from_right), other))
    share.wait_recv()
    for copy in forward:
        copy.wait_recv()
    for copy in copies:
        copy.wait_send()
    keep.wait()


def gather_queries(queries):
    piece = (4, STEP, WIDTH)
    return pl.pallas_call(
        gather_kernel,
        out_shape=jax.ShapeDtypeStruct((4, *piece), jnp.bfloat16),
        in_specs=[pl.BlockSpec(memory_space=pl.ANY)],
        out_specs=pl.BlockSpec(memory_space=pl.ANY),
        scratch_shapes=[
            pltpu.SemaphoreType.DMA,
            pltpu.SemaphoreType.DMA((9,)),
            pltpu.SemaphoreType.DMA((9,)),
        ],
        compiler_params=pltpu.CompilerParams(
            collective_id=0, has_side_effects=True, vmem_limit_bytes=4 << 20
        ),
        name="gather_queries",
    )(queries.reshape(piece))


def attend_kernel(
    branch, queries, keys, values, step_keys, step_values, out, stats, peak, total, mixed
):
    blk = lax.axis_index("blk")
    quarter = lax.axis_index("quarter")
    chunk = blk * 8 + quarter
    count = keys.shape[0]
    start = chunk * count
    rows = GROUP * STEP
    factor = HD ** (-0.5) * LOG2E

    def one(p, _):
        seen = jnp.clip(branch[p] - start, 0, count)
        blocks = (seen + KEY_BLOCK - 1) // KEY_BLOCK
        query = jnp.concatenate(
            [queries[p, :, h * HD : (h + 1) * HD] for h in range(GROUP)], axis=0
        )
        peak[...] = jnp.full((rows, HD), NEGATIVE, jnp.float32)
        total[...] = jnp.zeros((rows, HD), jnp.float32)
        mixed[...] = jnp.zeros((rows, HD), jnp.float32)

        def absorb(scores, value):
            old = peak[:, 0:1]
            new = jnp.maximum(old, jnp.max(scores, axis=1, keepdims=True))
            weight = jnp.exp2(scores - new)
            shrink = jnp.exp2(old - new)
            width = weight.shape[1]
            if width >= HD:
                part = weight[:, 0:HD]
                for i in range(1, width // HD):
                    part = part + weight[:, i * HD : (i + 1) * HD]
                total[...] = total[...] * shrink + part
            else:
                first = lax.broadcasted_iota(jnp.int32, (rows, HD), 1) == 0
                sum_ = jnp.sum(weight, axis=1, keepdims=True)
                total[...] = total[...] * shrink + jnp.where(first, sum_, 0.0)
            mixed[...] = mixed[...] * shrink + jnp.dot(
                weight.astype(jnp.bfloat16), value, preferred_element_type=jnp.float32
            )
            peak[...] = jnp.broadcast_to(new, (rows, HD))

        def block(b, _):
            at = pl.multiple_of(b * KEY_BLOCK, KEY_BLOCK)
            key = keys[pl.ds(at, KEY_BLOCK), :]
            scores = lax.dot_general(
                query, key, (((1,), (1,)), ((), ())), preferred_element_type=jnp.float32
            )
            index = at + lax.broadcasted_iota(jnp.int32, (1, KEY_BLOCK), 1)
            scores = jnp.where(index < seen, scores * factor, NEGATIVE)
            absorb(scores, values[pl.ds(at, KEY_BLOCK), :])
            return 0

        lax.fori_loop(0, blocks, block, 0)

        @pl.when(p == chunk - PARTICLES)
        def _():
            at = pl.multiple_of(p * STEP, STEP)
            key = step_keys[pl.ds(at, STEP), :]
            scores = lax.dot_general(
                query, key, (((1,), (1,)), ((), ())), preferred_element_type=jnp.float32
            )
            token = lax.broadcasted_iota(jnp.int32, (rows, STEP), 0) % STEP
            fresh = lax.broadcasted_iota(jnp.int32, (rows, STEP), 1)
            scores = jnp.where(fresh <= token, scores * factor, NEGATIVE)
            absorb(scores, step_values[pl.ds(at, STEP), :])

        sums = jnp.sum(total[...], axis=1, keepdims=True)
        some = sums > 0.0
        safe = jnp.where(some, sums, 1.0)
        result = (mixed[...] / safe).astype(jnp.bfloat16)
        level = jnp.where(some, peak[:, 0:1] + jnp.log2(safe), NEGATIVE)
        for h in range(GROUP):
            out[p, :, h * HD : (h + 1) * HD] = result[h * STEP : (h + 1) * STEP, :]
        lane = lax.broadcasted_iota(jnp.int32, (8, HD), 1)
        for half in range(2):
            tile = jnp.full((8, HD), NEGATIVE, jnp.float32)
            for h in range(HEADS):
                at = (half * HEADS + h) * STEP
                for j in range(2):
                    tile = jnp.where(
                        lane == j * HEADS + h, level[at + j * 8 : at + j * 8 + 8, :], tile
                    )
            stats[half, p] = tile
        return 0

    lax.fori_loop(0, PARTICLES, one, 0)


def attend(branch, queries, keys, values, step_keys, step_values):
    vmem = pl.BlockSpec(memory_space=pltpu.VMEM)
    rows = GROUP * STEP
    return pl.pallas_call(
        attend_kernel,
        out_shape=(
            jax.ShapeDtypeStruct((PARTICLES, STEP, WIDTH), jnp.bfloat16),
            jax.ShapeDtypeStruct((2, PARTICLES, 8, HD), jnp.float32),
        ),
        in_specs=[pl.BlockSpec(memory_space=pltpu.SMEM)] + [vmem] * 5,
        out_specs=(vmem, vmem),
        scratch_shapes=[pltpu.VMEM((rows, HD), jnp.float32)] * 3,
        compiler_params=pltpu.CompilerParams(vmem_limit_bytes=24 << 20),
        name="attend",
    )(branch, queries, keys, values, step_keys, step_values)


def spread(tile, h):
    return [
        jnp.broadcast_to(tile[:, j * HEADS + h : j * HEADS + h + 1], (8, HD)) for j in range(2)
    ]


def weigh(shares, parts, h):
    sums = None
    for share, part in zip(shares, parts, strict=True):
        scale = jnp.concatenate(spread(share, h), axis=0)
        sums = part * scale if sums is None else sums + part * scale
    return sums


def finish_kernel(
    partial,
    stats,
    weight,
    out,
    weight_v,
    own,
    own_stats,
    twin,
    twin_stats,
    chip,
    chip_stats,
    landed,
    landed_stats,
    attended,
    shares,
    zone,
    local_sem,
    pair_send,
    pair_recv,
    data_send,
    data_recv,
    stat_send,
    stat_recv,
    all_send,
    all_recv,
    forward_send,
    forward_recv,
    zone_send,
    zone_recv,
):
    head, x, y, core = place()
    other = device(head, x, y, 1 - core)
    mine = x * 4 + y

    def chip_at(i):
        there_x, there_y = (x + i // 4) % 4, (y + i % 4) % 4
        return device(head, there_x, there_y, core), there_x * 4 + there_y

    def head_at(i):
        return device((head + i) % 8, x, y, core), (head + i) % 8

    barrier = pltpu.get_barrier_semaphore()
    pl.semaphore_signal(barrier, inc=1, device_id=other, device_id_type=MESH)
    for i in range(1, 16):
        pl.semaphore_signal(barrier, inc=1, device_id=chip_at(i)[0], device_id_type=MESH)
    for i in range(1, 8):
        pl.semaphore_signal(barrier, inc=1, device_id=head_at(i)[0], device_id_type=MESH)
    my_half = pl.ds(pl.multiple_of(core * HALF, HALF), HALF)
    its_half = pl.ds(pl.multiple_of((1 - core) * HALF, HALF), HALF)
    load_weight = pltpu.make_async_copy(weight, weight_v, local_sem.at[0])
    load_own = pltpu.make_async_copy(partial.at[:, :, my_half], own, local_sem.at[1])
    load_stats = pltpu.make_async_copy(stats.at[core], own_stats, local_sem.at[2])
    load_own.start()
    load_stats.start()
    load_weight.start()
    pl.semaphore_wait(barrier, 23)

    to_twin = [
        remote(partial.at[:, :, its_half], twin, pair_send.at[0], pair_recv.at[0], other),
        remote(stats.at[1 - core], twin_stats, pair_send.at[1], pair_recv.at[1], other),
    ]
    for copy in to_twin:
        copy.start()
    load_own.wait()
    load_stats.wait()
    for copy in to_twin:
        copy.wait_recv()

    def send_chip(i):
        to, p = chip_at(i)
        return (
            remote(chip.at[p], landed.at[i], data_send.at[i], data_recv.at[i], to),
            remote(chip_stats.at[p], landed_stats.at[i], stat_send.at[i], stat_recv.at[i], to),
        )

    def pair(p):
        a, b = own_stats[p], twin_stats[p]
        top = jnp.maximum(a, b)
        wa, wb = jnp.exp2(a - top), jnp.exp2(b - top)
        both = wa + wb
        chip_stats[p] = top + jnp.log2(both)
        wa, wb = wa / both, wb / both
        for h in range(HEADS):
            cols = slice(h * HD, (h + 1) * HD)
            parts = [own[p, :, cols].astype(jnp.float32), twin[p, :, cols].astype(jnp.float32)]
            chip[p, :, cols] = weigh((wa, wb), parts, h).astype(jnp.bfloat16)

    def pair_step(k, _):
        i = 15 - k
        pair(chip_at(i)[1])
        for copy in send_chip(i):
            copy.start()
        return 0

    lax.fori_loop(0, 15, pair_step, 0)
    pair(mine)
    landed[0] = chip[mine]
    landed_stats[0] = chip_stats[mine]

    def landed_step(i, _):
        for copy in send_chip(i):
            copy.wait_recv()
        return 0

    lax.fori_loop(1, 16, landed_step, 0)
    top = landed_stats[0]
    for i in range(1, 16):
        top = jnp.maximum(top, landed_stats[i])
    sums = jnp.zeros((8, HD), jnp.float32)
    for i in range(16):
        share = jnp.exp2(landed_stats[i] - top)
        shares[i] = share
        sums = sums + share
    inverse = 1.0 / sums
    for h in range(HEADS):
        cols = slice(h * HD, (h + 1) * HD)
        weights = [shares[i] * inverse for i in range(16)]
        parts = [landed[i, :, cols].astype(jnp.float32) for i in range(16)]
        attended[mine, :, pl.ds(pl.multiple_of(core * HALF + h * HD, HD), HD)] = weigh(
            weights, parts, h
        ).astype(jnp.bfloat16)

    def send_all(i):
        ref = attended.at[mine, :, my_half]
        return remote(ref, ref, all_send.at[i], all_recv.at[i], chip_at(i)[0])

    def forward(i):
        p = ((x + 4 - i // 4) % 4) * 4 + (y + 4 - i % 4) % 4
        ref = attended.at[p, :, my_half]
        return remote(ref, ref, forward_send.at[i], forward_recv.at[i], other)

    def all_step(k, _):
        send_all(15 - k).start()
        return 0

    lax.fori_loop(0, 15, all_step, 0)
    forward(0).start()

    def forward_step(i, _):
        send_all(i).wait_recv()
        forward(i).start()
        return 0

    lax.fori_loop(1, 16, forward_step, 0)

    def forwarded_step(i, _):
        forward(i).wait_recv()
        return 0

    lax.fori_loop(0, 16, forwarded_step, 0)
    load_weight.wait()

    def project(g, _):
        rows = attended[pl.ds(g * 8, 8)].reshape(8 * STEP, WIDTH)
        result = jnp.dot(rows, weight_v[...], preferred_element_type=jnp.float32)
        shares_out = result.astype(jnp.bfloat16).reshape(4, 2 * STEP, -1)
        zone[pl.ds(g * 4, 4)] = shares_out
        return 0

    lax.fori_loop(0, 2, project, 0)

    def send_zone(i):
        to, h = head_at(i)
        return remote(zone.at[h], zone.at[8 + i], zone_send.at[i], zone_recv.at[i], to)

    def zone_step(k, _):
        send_zone(lax.rem(k + 3, 7) + 1).start()
        return 0

    lax.fori_loop(0, 7, zone_step, 0)
    result = zone[head].astype(jnp.float32)
    for i in range(1, 8):
        send_zone(i).wait_recv()
        result = result + zone[8 + i].astype(jnp.float32)
    out[...] = result.astype(jnp.bfloat16)

    for copy in to_twin:
        copy.wait_send()

    def drain(i, _):
        for copy in send_chip(i):
            copy.wait_send()
        send_all(i).wait_send()
        forward(i).wait_send()
        return 0

    lax.fori_loop(1, 16, drain, 0)
    forward(0).wait_send()
    for i in range(1, 8):
        send_zone(i).wait_send()


def finish(partial, stats, weight):
    any_ = pl.BlockSpec(memory_space=pl.ANY)
    width = weight.shape[1]
    dma = pltpu.SemaphoreType.DMA
    return pl.pallas_call(
        finish_kernel,
        out_shape=jax.ShapeDtypeStruct((2 * STEP, width), jnp.bfloat16),
        in_specs=[any_, any_, any_],
        out_specs=pl.BlockSpec(memory_space=pltpu.VMEM),
        scratch_shapes=[
            pltpu.VMEM(weight.shape, jnp.bfloat16),
            pltpu.VMEM((PARTICLES, STEP, HALF), jnp.bfloat16),
            pltpu.VMEM((PARTICLES, 8, HD), jnp.float32),
            pltpu.VMEM((PARTICLES, STEP, HALF), jnp.bfloat16),
            pltpu.VMEM((PARTICLES, 8, HD), jnp.float32),
            pltpu.VMEM((PARTICLES, STEP, HALF), jnp.bfloat16),
            pltpu.VMEM((PARTICLES, 8, HD), jnp.float32),
            pltpu.VMEM((16, STEP, HALF), jnp.bfloat16),
            pltpu.VMEM((16, 8, HD), jnp.float32),
            pltpu.VMEM((PARTICLES, STEP, WIDTH), jnp.bfloat16),
            pltpu.VMEM((16, 8, HD), jnp.float32),
            pltpu.VMEM((16, 2 * STEP, width), jnp.bfloat16),
            dma((3,)),
            dma((2,)),
            dma((2,)),
            dma((16,)),
            dma((16,)),
            dma((16,)),
            dma((16,)),
            dma((16,)),
            dma((16,)),
            dma((16,)),
            dma((16,)),
            dma((8,)),
            dma((8,)),
        ],
        compiler_params=pltpu.CompilerParams(
            collective_id=1, has_side_effects=True, vmem_limit_bytes=24 << 20
        ),
        name="finish",
    )(partial, stats, weight)


def body(queries, cache_keys, cache_values, step_keys, step_values, branch, out_weight):
    everyone = gather_queries(queries).reshape(PARTICLES, STEP, WIDTH)
    partial, stats = attend(
        branch,
        everyone,
        cache_keys[:, 0],
        cache_values[:, 0],
        step_keys[:, 0],
        step_values[:, 0],
    )
    return finish(partial, stats, out_weight)


def solution(mesh):
    every = ("blk", "quarter")
    placed = (
        P("blk", "head"),
        P(every, "head", None),
        P(every, "head", None),
        P(None, "head", None),
        P(None, "head", None),
        P(),
        P("head", every),
    )
    return jax.shard_map(
        body, mesh=mesh, in_specs=placed, out_specs=P("head", every), check_vma=False
    )
```

```python
import functools

import jax
import jax.numpy as jnp
from jax import lax
from jax.experimental import pallas as pl
from jax.experimental.pallas import tpu as pltpu
from jax.sharding import PartitionSpec as P

MESH = pl.DeviceIdType.MESH
NEGATIVE = -1e30
LOG2E = 1.4426950408889634
PARTICLES = 16
STEP = 16
GROUP = 16
HD = 128
WIDTH = GROUP * HD
HALF = WIDTH // 2
HEADS = 8
KEY_BLOCK = 512
TOGETHER = 4


def place():
    head = lax.axis_index("head")
    blk = lax.axis_index("blk")
    quarter = lax.axis_index("quarter")
    return head, quarter // 2, (blk // 2) * 2 + quarter % 2, blk % 2


def device(head, x, y, core):
    return (head, (y // 2) * 2 + core, x * 2 + y % 2)


def remote(src, dst, send, recv, to):
    return pltpu.make_async_remote_copy(
        src_ref=src,
        dst_ref=dst,
        send_sem=send,
        recv_sem=recv,
        device_id=to,
        device_id_type=MESH,
    )


def gather_kernel(
    mine,
    key,
    value,
    step_key,
    step_value,
    branch,
    everyone,
    keys,
    values,
    step_keys,
    step_values,
    branches,
    local_sem,
    pair_send,
    pair_recv,
    send,
    recv,
):
    head, x, y, core = place()
    other = device(head, x, y, 1 - core)
    across = [device(head, x, 3 - y, c) for c in range(2)]
    right = device(head, (x + 1) % 4, y, core)
    left = device(head, (x + 3) % 4, y, core)
    barrier = pltpu.get_barrier_semaphore()
    for peer in (other, *across, right, left):
        pl.semaphore_signal(barrier, inc=1, device_id=peer, device_id_type=MESH)

    def half(c):
        return pl.ds(pl.multiple_of(c * HALF, HALF), HALF)

    own_block = (y // 2) * 2 + core
    own_rows = pl.ds(own_block * 4, 4)
    local = [
        pltpu.make_async_copy(mine.at[:, :, half(core)], everyone.at[own_rows], local_sem.at[0]),
        pltpu.make_async_copy(key, keys.at[core], local_sem.at[1]),
        pltpu.make_async_copy(value, values.at[core], local_sem.at[2]),
        pltpu.make_async_copy(step_key, step_keys, local_sem.at[3]),
        pltpu.make_async_copy(step_value, step_values, local_sem.at[4]),
        pltpu.make_async_copy(branch, branches, local_sem.at[5]),
    ]
    pl.semaphore_wait(barrier, 5)
    direct = []
    for k, piece in enumerate((x, (x + 2) % 4)):
        for c in range(2):
            copy = remote(
                mine.at[piece, :, half(c)],
                everyone.at[own_block * 4 + piece],
                send.at[c * 2 + k],
                recv.at[core * 2 + k],
                across[c],
            )
            copy.start()
            direct.append(copy)
    pair = [
        remote(src, dst, pair_send.at[i], pair_recv.at[i], other)
        for i, (src, dst) in enumerate(
            (
                (mine.at[:, :, half(1 - core)], everyone.at[own_rows]),
                (key, keys.at[core]),
                (value, values.at[core]),
            )
        )
    ]
    for copy in pair:
        copy.start()
    for copy in local:
        copy.start()

    def far(c, piece):
        return everyone.at[((1 - y // 2) * 2 + c) * 4 + piece]

    def landing(c, k):
        ref = far(c, (x + 2 * k) % 4)
        return remote(ref, ref, send.at[c * 2 + k], recv.at[c * 2 + k], across[c])

    passed = []
    for c in range(2):
        landing(c, 0).wait_recv()
        for side, to in enumerate((right, left)):
            index = 4 + side * 2 + c
            copy = remote(far(c, x), far(c, x), send.at[index], recv.at[index], to)
            copy.start()
            passed.append(copy)
    for c in range(2):
        landing(c, 1).wait_recv()
    for copy in pair:
        copy.wait_recv()
    for copy in local:
        copy.wait()
    for copy in passed:
        copy.wait_recv()
    for copy in direct + pair + passed:
        copy.wait_send()


def gather_queries(queries, key, value, step_key, step_value, branch):
    hbm = pl.BlockSpec(memory_space=pltpu.HBM)
    any_ = pl.BlockSpec(memory_space=pl.ANY)
    count = key.shape[0]
    bf16 = jnp.bfloat16
    return pl.pallas_call(
        gather_kernel,
        out_shape=(
            jax.ShapeDtypeStruct((PARTICLES, STEP, HALF), bf16),
            jax.ShapeDtypeStruct((2, count, HD), bf16),
            jax.ShapeDtypeStruct((2, count, HD), bf16),
            jax.ShapeDtypeStruct(step_key.shape, bf16),
            jax.ShapeDtypeStruct(step_value.shape, bf16),
            jax.ShapeDtypeStruct(branch.shape, branch.dtype),
        ),
        in_specs=[hbm] * 6,
        out_specs=(any_,) * 6,
        scratch_shapes=[
            pltpu.SemaphoreType.DMA((6,)),
            pltpu.SemaphoreType.DMA((3,)),
            pltpu.SemaphoreType.DMA((3,)),
            pltpu.SemaphoreType.DMA((8,)),
            pltpu.SemaphoreType.DMA((8,)),
        ],
        compiler_params=pltpu.CompilerParams(
            collective_id=0, has_side_effects=True, vmem_limit_bytes=4 << 20
        ),
        name="gather_queries",
    )(
        *(
            pltpu.with_memory_space_constraint(a, pltpu.HBM)
            for a in (queries.reshape(4, STEP, WIDTH), key, value, step_key, step_value, branch)
        )
    )


def owned(head, x, y):
    return ((x + head // 2) % 4) * 4 + y


def attend_kernel(
    branch,
    queries,
    keys,
    values,
    step_keys,
    step_values,
    out,
    stats,
    order,
    query,
    peak,
    total,
    mixed,
):
    head, x, y, core = place()
    count = keys.shape[1]
    first_chunk = (y // 2) * 16 + x * 2 + y % 2
    first_start = first_chunk * count
    mine = owned(head, x, y)
    size = HEADS * STEP
    factor = HD ** (-0.5) * LOG2E

    limits = [branch[i] for i in range(PARTICLES)]
    for i in range(PARTICLES):
        rank = 0
        for j in range(PARTICLES):
            if j != i:
                ahead = limits[j] >= limits[i] if j < i else limits[j] > limits[i]
                rank = rank + ahead.astype(jnp.int32)
        order[rank] = i

    def absorb(rows, scores, value):
        old = peak[rows, 0:1]
        new = jnp.maximum(old, jnp.max(scores, axis=1, keepdims=True))
        weight = jnp.exp2(scores - new)
        shrink = jnp.exp2(old - new)
        width = weight.shape[1]
        if width >= HD:
            part = weight[:, 0:HD]
            for i in range(1, width // HD):
                part = part + weight[:, i * HD : (i + 1) * HD]
        else:
            lane = lax.broadcasted_iota(jnp.int32, (weight.shape[0], HD), 1)
            part = jnp.where(lane == 0, jnp.sum(weight, axis=1, keepdims=True), 0.0)
        total[rows] = total[rows] * shrink + part
        mixed[rows] = mixed[rows] * shrink + jnp.dot(
            weight.astype(jnp.bfloat16), value, preferred_element_type=jnp.float32
        )
        peak[rows] = jnp.broadcast_to(new, (weight.shape[0], HD))

    def product(rows, key):
        return lax.dot_general(
            query[rows, :], key, (((1,), (1,)), ((), ())), preferred_element_type=jnp.float32
        )

    def some_blocks(part, seen, together):
        rows = slice(0, together * size)

        def block(b, _):
            at = pl.multiple_of(b * KEY_BLOCK, KEY_BLOCK)
            scores = product(rows, keys[part, pl.ds(at, KEY_BLOCK), :])
            index = at + lax.broadcasted_iota(jnp.int32, (1, KEY_BLOCK), 1)
            scores = jnp.concatenate(
                [
                    jnp.where(
                        index < seen[k], scores[k * size : (k + 1) * size] * factor, NEGATIVE
                    )
                    for k in range(together)
                ],
                axis=0,
            )
            absorb(rows, scores, values[part, pl.ds(at, KEY_BLOCK), :])
            return 0

        lax.fori_loop(0, (seen[0] + KEY_BLOCK - 1) // KEY_BLOCK, block, 0)

    def fresh_block(k):
        rows = pl.ds(k * size, size)
        at = pl.multiple_of(mine * STEP, STEP)
        scores = product(rows, step_keys[pl.ds(at, STEP), :])
        token = lax.broadcasted_iota(jnp.int32, (size, STEP), 0) % STEP
        fresh = lax.broadcasted_iota(jnp.int32, (size, STEP), 1)
        scores = jnp.where(fresh <= token, scores * factor, NEGATIVE)
        absorb(rows, scores, step_values[pl.ds(at, STEP), :])

    lane = lax.broadcasted_iota(jnp.int32, (8, HD), 1)

    def group(g, _):
        ids = [order[g * TOGETHER + k] for k in range(TOGETHER)]
        ends = [branch[p] for p in ids]
        active = ends[0] > first_start
        for p in ids:
            active = jnp.logical_or(active, p == mine)

        @pl.when(active)
        def _():
            for k, p in enumerate(ids):
                for h in range(HEADS):
                    at = k * size + h * STEP
                    query[at : at + STEP, :] = queries[p, :, h * HD : (h + 1) * HD]
            peak[...] = jnp.full(peak.shape, NEGATIVE, jnp.float32)
            total[...] = jnp.zeros(total.shape, jnp.float32)
            mixed[...] = jnp.zeros(mixed.shape, jnp.float32)

            def part_step(part, _):
                start = first_start + part * 8 * count
                seen = [jnp.clip(end - start, 0, count) for end in ends]

                @pl.when(seen[1] > 0)
                def _():
                    some_blocks(part, seen, TOGETHER)

                @pl.when(seen[1] <= 0)
                def _():
                    some_blocks(part, seen, 1)

                return 0

            lax.fori_loop(0, 2, part_step, 0)
            for k, p in enumerate(ids):

                @pl.when(p == mine)
                def _(k=k):
                    fresh_block(k)

            sums = jnp.sum(total[...], axis=1, keepdims=True)
            some = sums > 0.0
            safe = jnp.where(some, sums, 1.0)
            result = (mixed[...] * (1.0 / safe)).astype(jnp.bfloat16)
            level = jnp.where(some, peak[...] + jnp.log2(safe), NEGATIVE)
            for k, p in enumerate(ids):
                tile = jnp.full((8, HD), NEGATIVE, jnp.float32)
                for h in range(HEADS):
                    at = k * size + h * STEP
                    out[p, :, h * HD : (h + 1) * HD] = result[at : at + STEP, :]
                    for j in range(2):
                        piece = level[at + j * 8 : at + j * 8 + 8, :]
                        tile = jnp.where(lane == j * HEADS + h, piece, tile)
                stats[p] = tile

        @pl.when(jnp.logical_not(active))
        def _():
            for p in ids:
                out[p] = jnp.zeros(out.shape[1:], jnp.bfloat16)
                stats[p] = jnp.full((8, HD), NEGATIVE, jnp.float32)

        return 0

    lax.fori_loop(0, PARTICLES // TOGETHER, group, 0)


def attend(branch, queries, keys, values, step_keys, step_values):
    vmem = pl.BlockSpec(memory_space=pltpu.VMEM)
    rows = TOGETHER * HEADS * STEP
    return pl.pallas_call(
        attend_kernel,
        out_shape=(
            jax.ShapeDtypeStruct((PARTICLES, STEP, HALF), jnp.bfloat16),
            jax.ShapeDtypeStruct((PARTICLES, 8, HD), jnp.float32),
        ),
        in_specs=[pl.BlockSpec(memory_space=pltpu.SMEM)] + [vmem] * 5,
        out_specs=(vmem, vmem),
        scratch_shapes=[
            pltpu.SMEM((PARTICLES,), jnp.int32),
            pltpu.VMEM((rows, HD), jnp.bfloat16),
        ]
        + [pltpu.VMEM((rows, HD), jnp.float32)] * 3,
        compiler_params=pltpu.CompilerParams(vmem_limit_bytes=24 << 20),
        name="attend",
    )(branch, queries, keys, values, step_keys, step_values)


def weigh(weights, parts, h):
    sums = None
    for weight, part in zip(weights, parts, strict=True):
        scale = jnp.concatenate(
            [
                jnp.broadcast_to(weight[:, j * HEADS + h : j * HEADS + h + 1], (8, HD))
                for j in range(2)
            ],
            axis=0,
        )
        term = part.astype(jnp.float32) * scale
        sums = term if sums is None else sums + term
    return sums


def finish_kernel(
    partial,
    stats,
    weight,
    out,
    landed,
    landed_stats,
    attended,
    leaving,
    arriving,
    data_send,
    data_recv,
    stat_send,
    stat_recv,
    all_send,
    all_recv,
    forward_send,
    forward_recv,
    zone_send,
    zone_recv,
):
    head, x, y, core = place()
    other = device(head, x, y, 1 - core)
    mine = owned(head, x, y)

    def chip_at(i):
        there_x, there_y = (x + i // 4) % 4, (y + i % 4) % 4
        return device(head, there_x, there_y, core), owned(head, there_x, there_y)

    def head_at(i):
        return device((head + i) % 8, x, y, core)

    barrier = pltpu.get_barrier_semaphore()
    for i in range(1, 16):
        pl.semaphore_signal(barrier, inc=1, device_id=chip_at(i)[0], device_id_type=MESH)
    pl.semaphore_signal(barrier, inc=1, device_id=other, device_id_type=MESH)
    for i in range(1, 8):
        pl.semaphore_signal(barrier, inc=1, device_id=head_at(i), device_id_type=MESH)
    pl.semaphore_wait(barrier, 23)

    def send_chip(i):
        to, p = chip_at(i)
        return (
            remote(partial.at[p], landed.at[i], data_send.at[i], data_recv.at[i], to),
            remote(stats.at[p], landed_stats.at[i], stat_send.at[i], stat_recv.at[i], to),
        )

    def chip_step(k, _):
        for copy in send_chip(15 - k):
            copy.start()
        return 0

    lax.fori_loop(0, 15, chip_step, 0)
    landed[0] = partial[mine]
    landed_stats[0] = stats[mine]

    def landed_step(i, _):
        for copy in send_chip(i):
            copy.wait_recv()
        return 0

    lax.fori_loop(1, 16, landed_step, 0)
    top = landed_stats[0]
    for i in range(1, 16):
        top = jnp.maximum(top, landed_stats[i])
    shares = [jnp.exp2(landed_stats[i] - top) for i in range(16)]
    inverse = 1.0 / functools.reduce(jnp.add, shares)
    shares = [share * inverse for share in shares]
    for h in range(HEADS):
        parts = [landed[i, :, h * HD : (h + 1) * HD] for i in range(16)]
        attended[mine, :, pl.ds(pl.multiple_of(core * HALF + h * HD, HD), HD)] = weigh(
            shares, parts, h
        ).astype(jnp.bfloat16)

    my_half = pl.ds(pl.multiple_of(core * HALF, HALF), HALF)

    def send_all(i):
        ref = attended.at[mine, :, my_half]
        return remote(ref, ref, all_send.at[i], all_recv.at[i], chip_at(i)[0])

    def forward(i):
        ref = attended.at[owned(head, (x + 4 - i // 4) % 4, (y + 4 - i % 4) % 4), :, my_half]
        return remote(ref, ref, forward_send.at[i], forward_recv.at[i], other)

    def column(k):
        return k ^ (k // 2)

    forward(0).start()

    def all_step(k, _):
        send_all(column(k // 4) * 4 + k % 4).start()
        return 0

    lax.fori_loop(1, 16, all_step, 0)

    def send_zone(i):
        return remote(
            leaving.at[(head + i) % 8], arriving.at[i], zone_send.at[i], zone_recv.at[i], head_at(i)
        )

    def project(k, _):
        dx = column(k)

        def take(j, _):
            @pl.when(dx * 4 + j > 0)
            def _():
                send_all(dx * 4 + j).wait_recv()
                forward(dx * 4 + j).start()

            return 0

        lax.fori_loop(0, 4, take, 0)

        def taken(j, _):
            forward(dx * 4 + j).wait_recv()
            return 0

        lax.fori_loop(0, 4, taken, 0)
        there = (x + 4 - dx + head // 2) % 4
        rows = attended[pl.ds(there * 4, 4)].reshape(4 * STEP, WIDTH)
        result = jnp.dot(rows, weight[...], preferred_element_type=jnp.float32)
        leaving[pl.ds(there * 2, 2)] = result.astype(jnp.bfloat16).reshape(2, 2 * STEP, -1)
        for j in range(2):
            offset = (there * 2 + j + 8 - head) % 8

            @pl.when(offset > 0)
            def _(offset=offset):
                send_zone(offset).start()

        return 0

    lax.fori_loop(0, 4, project, 0)
    result = leaving[head].astype(jnp.float32)
    for i in range(1, 8):
        send_zone(i).wait_recv()
        result = result + arriving[i].astype(jnp.float32)
    out[...] = result.astype(jnp.bfloat16)

    def drain(i, _):
        for copy in send_chip(i):
            copy.wait_send()
        send_all(i).wait_send()
        forward(i).wait_send()
        return 0

    lax.fori_loop(1, 16, drain, 0)
    forward(0).wait_send()
    for i in range(1, 8):
        send_zone(i).wait_send()


def finish(partial, stats, weight):
    vmem = pl.BlockSpec(memory_space=pltpu.VMEM)
    width = weight.shape[1]
    dma = pltpu.SemaphoreType.DMA
    return pl.pallas_call(
        finish_kernel,
        out_shape=jax.ShapeDtypeStruct((2 * STEP, width), jnp.bfloat16),
        in_specs=[vmem] * 3,
        out_specs=vmem,
        scratch_shapes=[
            pltpu.VMEM((16, STEP, HALF), jnp.bfloat16),
            pltpu.VMEM((16, 8, HD), jnp.float32),
            pltpu.VMEM((PARTICLES, STEP, WIDTH), jnp.bfloat16),
            pltpu.VMEM((8, 2 * STEP, width), jnp.bfloat16),
            pltpu.VMEM((8, 2 * STEP, width), jnp.bfloat16),
        ]
        + [dma((16,))] * 8
        + [dma((8,))] * 2,
        compiler_params=pltpu.CompilerParams(
            collective_id=1, has_side_effects=True, vmem_limit_bytes=24 << 20
        ),
        name="finish",
    )(partial, stats, weight)


def body(queries, cache_keys, cache_values, step_keys, step_values, branch, out_weight):
    *gathered, branches = gather_queries(
        queries, cache_keys[:, 0], cache_values[:, 0], step_keys[:, 0], step_values[:, 0], branch
    )
    partial, stats = attend(branches, *gathered)
    return finish(partial, stats, out_weight)


def solution(mesh):
    every = ("blk", "quarter")
    placed = (
        P("blk", "head"),
        P(every, "head", None),
        P(every, "head", None),
        P(None, "head", None),
        P(None, "head", None),
        P(),
        P("head", every),
    )
    return jax.shard_map(
        body, mesh=mesh, in_specs=placed, out_specs=P("head", every), check_vma=False
    )
```
